32 devices in a mesh: cuts: 4 (over z), tile: 2 (over core), probe: 4 (over y, x).
Axes of the slice: x: 2, y: 2, z: 4, core: 2. Of those that a mesh axis runs over, the one named last changes fastest.
Arguments:
- probe_wave: bfloat16 [2, 512, 512], replicated, may hold values from -6 to 6
- fresnel_rows: bfloat16 [2, 512, 512], replicated, may hold values from -0.1875 to 0.1875
- fresnel_cols: bfloat16 [2, 512, 512], replicated, may hold values from -0.1875 to 0.1875
- object_slices: float32 [4, 2, 1024, 768], P('cuts', None, 'tile'), may hold values from -1 to 1.9, as said below
- offsets: int32 [2, 8, 2], P('tile', 'probe'), may hold values from 0 to 256
- measured: float32 [2, 8, 512, 512], P('tile', 'probe'), may hold values from 0.2 to 2
Outputs:
- updated_object: float32 [4, 2, 1024, 768], P('cuts', None, ('tile', 'probe'))
The draws below stay inside these ranges and needn't reach their ends.
Inputs may be any that keep to these rules, and one draw needn't show every extreme that they name: `object_slices`: real and imaginary parts of each slice's transmission.
All inputs are finite; a program needn't handle non-finite values.
Results may differ from the reference program's by a relative error of at most 0.02.
Values may be sent and summed in bfloat16 or wider, within the bound.
No kernel may reach another device: no remote copies, remote signals or barrier semaphores. Data moves between devices by JAX's collectives and lax.ppermute only.
A program may use at most 128 MiB of HBM per device.

```python
import jax
import jax.numpy as jnp
from jax import lax

WINDOW = 512
MARGIN = 128
OWN_ROWS = 512
COLS = 768
ROWS = 1024
SLICES = 4
POSITIONS = 8
N_TILE = 2


def draw_object_slices(key, part):
    dimensions = (SLICES, 2, ROWS, COLS)
    jitter = jnp.clip(0.25 * jax.random.normal(key, dimensions, jnp.float32), -1.0, 1.0)
    center_value = jnp.array([0.9, 0.0], jnp.float32).reshape(1, 2, 1, 1)
    return center_value + jitter


def draw_offsets(key, part):
    row_key = jax.random.fold_in(key, 11)
    col_key = jax.random.fold_in(key, 23)
    row_most = OWN_ROWS + 2 * MARGIN - WINDOW
    col_most = 2 * MARGIN
    row_part = jax.random.randint(row_key, (N_TILE, POSITIONS), 0, row_most + 1, jnp.int32)
    col_part = jax.random.randint(col_key, (N_TILE, POSITIONS), 0, col_most + 1, jnp.int32)
    row_part = row_part.at[:, 0].set(row_most).at[:, 1].set(0)
    col_part = col_part.at[:, 0].set(col_most)
    return jnp.stack([row_part, col_part], axis=2).astype(jnp.int32)


def levels(stream_key, shape, shards, least, top_value):
    def one(dim, parts):
        heights = jax.random.uniform(jax.random.fold_in(jax.random.fold_in(stream_key, 6), dim), (parts,), jnp.float32, least / len(shards), top_value / len(shards))
        return jnp.repeat(jnp.exp(heights), shape[dim] // parts).reshape((-1,) + (1,) * (len(shape) - dim - 1))

    level = one(*shards[0])
    for cut in shards[1:]:
        level = level * one(*cut)
    return level


def gaussian(own_key, shape, width, limit, kind=jnp.bfloat16):
    values = jax.random.normal(own_key, shape, jnp.float32) * width
    return jnp.minimum(jnp.maximum(values, -limit), limit).astype(kind)


def setup_inputs(seed: int = 0) -> dict:
    seeds = jax.random.split(jax.random.key(seed), 7)
    probe_wave = gaussian(seeds[0], (2, WINDOW, WINDOW), 1.0, 6.0)
    fresnel_rows = gaussian(seeds[1], (2, WINDOW, WINDOW), (2 * WINDOW) ** -0.5, 0.1875)
    fresnel_cols = gaussian(seeds[2], (2, WINDOW, WINDOW), (2 * WINDOW) ** -0.5, 0.1875)
    object_slices = draw_object_slices(jax.random.fold_in(seeds[6], 71), 0)
    offsets = draw_offsets(jax.random.fold_in(seeds[6], 71), 0)
    measured = jnp.clip(0.2 + 1.8 * jax.random.uniform(seeds[5], (N_TILE, POSITIONS, WINDOW, WINDOW), jnp.float32) ** levels(seeds[5], (N_TILE, POSITIONS, WINDOW, WINDOW), ((0, 2), (1, 4)), -0.2, 0.2), 0.2, 2.0)
    return {"probe_wave": probe_wave, "fresnel_rows": fresnel_rows, "fresnel_cols": fresnel_cols, "object_slices": object_slices, "offsets": offsets, "measured": measured}


def right_product(wave_part, matrix):
    return jnp.einsum('mij,jk->mik', wave_part.astype(jnp.float32), matrix.astype(jnp.float32))

def left_product(matrix, wave_part):
    return jnp.einsum('ij,mjk->mik', matrix.astype(jnp.float32), wave_part.astype(jnp.float32))

def propagate(wave, rows_matrix, cols_matrix):
    real_in, imag_in = (wave[:, 0], wave[:, 1])
    col_real, col_imag = (cols_matrix[0].T, cols_matrix[1].T)
    mid_real = right_product(real_in, col_real) - right_product(imag_in, col_imag)
    mid_imag = right_product(real_in, col_imag) + right_product(imag_in, col_real)
    middle = jnp.stack([mid_real, mid_imag], axis=1).astype(jnp.bfloat16)
    row_real, row_imag = (rows_matrix[0], rows_matrix[1])
    out_real = left_product(row_real, middle[:, 0]) - left_product(row_imag, middle[:, 1])
    out_imag = left_product(row_imag, middle[:, 0]) + left_product(row_real, middle[:, 1])
    return jnp.stack([out_real, out_imag], axis=1).astype(jnp.bfloat16)

def adjoint(wave, rows_matrix, cols_matrix):
    real_in, imag_in = (wave[:, 0], wave[:, 1])
    col_real, col_imag = (cols_matrix[0], cols_matrix[1])
    mid_real = right_product(real_in, col_real) + right_product(imag_in, col_imag)
    mid_imag = right_product(imag_in, col_real) - right_product(real_in, col_imag)
    middle = jnp.stack([mid_real, mid_imag], axis=1).astype(jnp.bfloat16)
    row_real, row_imag = (rows_matrix[0].T, rows_matrix[1].T)
    out_real = left_product(row_real, middle[:, 0]) + left_product(row_imag, middle[:, 1])
    out_imag = left_product(row_real, middle[:, 1]) - left_product(row_imag, middle[:, 0])
    return jnp.stack([out_real, out_imag], axis=1).astype(jnp.bfloat16)

def complex_mul(left_side, right_side):
    return jnp.stack([left_side[:, 0] * right_side[:, 0] - left_side[:, 1] * right_side[:, 1], left_side[:, 0] * right_side[:, 1] + left_side[:, 1] * right_side[:, 0]], axis=1)

def conj_mul(left_side, right_side):
    return jnp.stack([left_side[:, 0] * right_side[:, 0] + left_side[:, 1] * right_side[:, 1], left_side[:, 0] * right_side[:, 1] - left_side[:, 1] * right_side[:, 0]], axis=1)

def reference(probe_wave, fresnel_rows, fresnel_cols, object_slices, offsets, measured):
    transmission = object_slices.astype(jnp.bfloat16)
    padded = jnp.concatenate([transmission[:, :, ROWS - MARGIN:], transmission, transmission[:, :, :MARGIN]], axis=2)
    tile_ids = jnp.arange(N_TILE, dtype=jnp.int32)
    row_starts = (tile_ids[:, None] * OWN_ROWS + offsets[:, :, 0]).reshape(-1).astype(jnp.int32)
    col_starts = offsets[:, :, 1].reshape(-1).astype(jnp.int32)
    total = N_TILE * POSITIONS

    def windows_of(slab):

        def cut_window(row_start, col_start):
            return lax.dynamic_slice(slab, (jnp.int32(0), row_start, col_start), (2, WINDOW, WINDOW))
        return jax.vmap(cut_window)(row_starts, col_starts)
    current = jnp.broadcast_to(probe_wave, (total, 2, WINDOW, WINDOW))
    stored_waves = []
    for slice_index in range(SLICES):
        stored_waves.append(current)
        windows = windows_of(padded[slice_index]).astype(jnp.float32)
        exits = complex_mul(current.astype(jnp.float32), windows).astype(jnp.bfloat16)
        current = propagate(exits, fresnel_rows, fresnel_cols)
    psi_final = current.astype(jnp.float32)
    amplitude = measured.reshape(total, WINDOW, WINDOW)
    factor = 1.0 - amplitude / jnp.sqrt(psi_final[:, 0] ** 2 + psi_final[:, 1] ** 2 + 1.0)
    cotangent = (psi_final * factor[:, None]).astype(jnp.bfloat16)
    results = [None] * SLICES
    for slice_index in reversed(range(SLICES)):
        backed = adjoint(cotangent, fresnel_rows, fresnel_cols).astype(jnp.float32)
        windows = windows_of(padded[slice_index]).astype(jnp.float32)
        incoming = stored_waves[slice_index].astype(jnp.float32)
        gradient_term = conj_mul(incoming, backed)
        intensity = incoming[:, 0] ** 2 + incoming[:, 1] ** 2
        cotangent = conj_mul(windows, backed).astype(jnp.bfloat16)
        pieces = jnp.concatenate([gradient_term, intensity[:, None]], axis=1)

        def add_piece(position, accum_grid):
            row_start = row_starts[position]
            col_start = col_starts[position]
            anchor = (jnp.int32(0), row_start, col_start)
            current_block = lax.dynamic_slice(accum_grid, anchor, (3, WINDOW, WINDOW))
            return lax.dynamic_update_slice(accum_grid, current_block + pieces[position], anchor)
        accum_grid = jnp.zeros((3, ROWS + 2 * MARGIN, COLS), jnp.float32)
        accum_grid = lax.fori_loop(0, total, add_piece, accum_grid)
        inside = accum_grid[:, MARGIN:MARGIN + ROWS]
        inside = inside.at[:, :MARGIN].add(accum_grid[:, MARGIN + ROWS:])
        inside = inside.at[:, ROWS - MARGIN:].add(accum_grid[:, :MARGIN])
        results[slice_index] = object_slices[slice_index] - inside[:2] / (inside[2] + 1.0)
    return jnp.stack(results, axis=0)
```

```python
import functools

import jax
import jax.numpy as jnp
from jax import lax
from jax.experimental import pallas as pl
from jax.experimental.pallas import tpu as pltpu
from jax.sharding import PartitionSpec as P

MARGIN = 128
F32 = jnp.float32
BF16 = jnp.bfloat16


def ring(count, by):
    return [(i, (i + by) % count) for i in range(count)]


def swapped(count, bit):
    return [(i, i ^ bit) for i in range(count)]


def spread(piece, bits):
    count = lax.axis_size("probe")
    held, order = piece[None], [0]
    for bit in bits:
        held = jnp.concatenate([held, lax.ppermute(held, "probe", swapped(count, bit))], axis=0)
        order = order + [j ^ bit for j in order]
    return held, order


def dot(a, b):
    return jnp.dot(a, b, preferred_element_type=F32)


CHUNK = 64
ALIGN = 16


def body(
    order_a,
    order_b,
    slice_count,
    info,
    starts,
    own,
    own_top,
    own_bottom,
    far_real,
    far_imag,
    far_top,
    far_bottom,
    probe,
    row_mat,
    row_mat_t,
    col_mat,
    col_mat_t,
    measured,
    out,
    stage,
    wins,
    saved,
    work,
    middle,
    wave,
    amplitude,
    probe_v,
    mats,
    grid,
    sem_stage,
    sem_mat,
    sem_in,
):
    size = probe_v.shape[1]
    count = wave.shape[0]
    own_rows = own.shape[1]
    lanes = size + 128
    mine, place = info[0], info[1]
    pieces = far_real.shape[1]
    piece_rows = own_rows // pieces
    col_last = (grid.shape[2] - size) // 128 - 1

    def stage_copies(k, act):
        slot = lax.rem(k, 2)
        sem = sem_stage.at[slot]

        def one(src, comp, first, rows):
            copy = pltpu.make_async_copy(src, stage.at[slot, comp, pl.ds(first, rows), :], sem)
            copy.start() if act else copy.wait()

        @pl.when(k == mine)
        def _():
            for comp in range(2):
                one(own_top.at[comp], comp, 0, MARGIN)
                one(own.at[comp], comp, MARGIN, own_rows)
                one(own_bottom.at[comp], comp, MARGIN + own_rows, MARGIN)

        @pl.when(k != mine)
        def _():
            far = lax.rem(mine - k + slice_count, slice_count) - 1
            for comp in range(2):
                source, order = ((far_real, order_a), (far_imag, order_b))[comp]
                one(far_top.at[far, comp], comp, 0, MARGIN)
                for j in range(pieces):
                    first = pl.multiple_of(MARGIN + (place ^ order[j]) * piece_rows, ALIGN)
                    one(source.at[far, j], comp, first, piece_rows)
                one(far_bottom.at[far, comp], comp, MARGIN + own_rows, MARGIN)

    mat_sources = (col_mat, row_mat, col_mat_t, row_mat_t)
    mat_copies = [
        pltpu.make_async_copy(source, mats.at[i], sem_mat.at[i])
        for i, source in enumerate(mat_sources)
    ]
    probe_copy = pltpu.make_async_copy(probe, probe_v, sem_in.at[0])
    measured_copy = pltpu.make_async_copy(measured, amplitude, sem_in.at[1])
    probe_copy.start()
    stage_copies(jnp.int32(0), True)
    for copy in mat_copies:
        copy.start()
    measured_copy.start()

    def clear(i, _):
        rows = pl.ds(pl.multiple_of(i * 8, 8), 8)
        for comp in range(3):
            grid[comp, rows, :] = jnp.zeros((8, grid.shape[2]), F32)
        return 0

    lax.fori_loop(0, grid.shape[1] // 8, clear, 0)
    probe_copy.wait()

    def fill(i, _):
        rows = pl.multiple_of(i * CHUNK, CHUNK)
        for comp in range(2):
            value = probe_v[comp, pl.ds(rows, CHUNK), :]
            for position in range(count):
                wave[position, pl.ds(rows + comp * size, CHUNK), :] = value
        return 0

    lax.fori_loop(0, size // CHUNK, fill, 0)

    def column(position):
        col = starts[position, 1]
        tile = jnp.minimum(col // 128, col_last)
        return pl.multiple_of(tile * 128, 128), col - tile * 128

    def add_piece(position, comp, i, value):
        row = starts[position, 0] + i * CHUNK
        inside = lax.rem(row, 8)
        first = pl.multiple_of(row - inside, 8)
        col_first, shift = column(position)
        wide = jnp.concatenate([value, jnp.zeros((CHUNK, 128), F32)], axis=1)
        wide = pltpu.roll(wide, shift, 1)
        tall = jnp.concatenate([wide, jnp.zeros((8, lanes), F32)], axis=0)
        tall = pltpu.roll(tall, inside, 0)
        grid[comp, pl.ds(first, CHUNK + 8), pl.ds(col_first, lanes)] += tall

    def halves(position, i):
        rows = pl.multiple_of(i * CHUNK, CHUNK)
        return (
            wave[position, pl.ds(rows, CHUNK), :].astype(F32),
            wave[position, pl.ds(rows + size, CHUNK), :].astype(F32),
        )

    def put_work(position, i, real, imag):
        rows = pl.ds(pl.multiple_of(i * CHUNK, CHUNK), CHUNK)
        work[position, rows, pl.ds(0, size)] = real.astype(BF16)
        work[position, rows, pl.ds(size, size)] = imag.astype(BF16)

    def propagate(position, col, row):
        for n in range(2):
            part = dot(work[position], mats[col, :, pl.ds(n * size, size)])
            middle[position, pl.ds(n * size, size), :] = part.astype(BF16)
        for m in range(2):
            part = dot(mats[row, pl.ds(m * size, size), :], middle[position])
            wave[position, pl.ds(m * size, size), :] = part.astype(BF16)

    def forward(k, _):
        slot = lax.rem(k, 2)
        stage_copies(k, False)

        @pl.when(k + 1 < slice_count)
        def _():
            stage_copies(k + 1, True)

        for position in range(count):
            row_start = starts[position, 0]
            col_first, shift = column(position)
            back_shift = lax.rem(lanes - shift, lanes)

            def enter(i, _):
                row = row_start + i * CHUNK
                inside = lax.rem(row, ALIGN)
                first = pl.multiple_of(row - inside, ALIGN)
                height = CHUNK + ALIGN

                def window(comp):
                    block = stage[
                        slot, comp, pl.ds(first, height), pl.ds(col_first, lanes)
                    ].astype(F32)
                    block = pltpu.roll(block, lax.rem(height - inside, height), 0)[:CHUNK]
                    return pltpu.roll(block, back_shift, 1)[:, :size]

                win_real, win_imag = window(0), window(1)
                rows = pl.ds(pl.multiple_of(i * CHUNK, CHUNK), CHUNK)
                wins[k, position, 0, rows, :] = win_real.astype(BF16)
                wins[k, position, 1, rows, :] = win_imag.astype(BF16)
                real, imag = halves(position, i)

                @pl.when(k == mine)
                def _():
                    saved[position, 0, rows, :] = real.astype(BF16)
                    saved[position, 1, rows, :] = imag.astype(BF16)
                    add_piece(position, 2, i, real * real + imag * imag)

                put_work(
                    position,
                    i,
                    real * win_real - imag * win_imag,
                    real * win_imag + imag * win_real,
                )
                return 0

            lax.fori_loop(0, size // CHUNK, enter, 0)

        @pl.when(k == 0)
        def _():
            mat_copies[0].wait()
            mat_copies[1].wait()

        for position in range(count):
            propagate(position, 0, 1)
        return 0

    lax.fori_loop(0, slice_count, forward, 0)
    measured_copy.wait()

    for position in range(count):

        def detect(i, _):
            real, imag = halves(position, i)
            seen = amplitude[position, pl.ds(pl.multiple_of(i * CHUNK, CHUNK), CHUNK), :]
            factor = 1.0 - seen / jnp.sqrt(real * real + imag * imag + 1.0)
            put_work(position, i, real * factor, imag * factor)
            return 0

        lax.fori_loop(0, size // CHUNK, detect, 0)

    mat_copies[2].wait()
    mat_copies[3].wait()

    def backward(step, _):
        k = slice_count - 1 - step
        for position in range(count):
            propagate(position, 2, 3)
        for position in range(count):

            def leave(i, _):
                rows = pl.ds(pl.multiple_of(i * CHUNK, CHUNK), CHUNK)
                real, imag = halves(position, i)

                @pl.when(k == mine)
                def _():
                    old_real = saved[position, 0, rows, :].astype(F32)
                    old_imag = saved[position, 1, rows, :].astype(F32)
                    add_piece(position, 0, i, old_real * real + old_imag * imag)
                    add_piece(position, 1, i, old_real * imag - old_imag * real)

                @pl.when(k != mine)
                def _():
                    win_real = wins[k, position, 0, rows, :].astype(F32)
                    win_imag = wins[k, position, 1, rows, :].astype(F32)
                    put_work(
                        position,
                        i,
                        win_real * real + win_imag * imag,
                        win_real * imag - win_imag * real,
                    )

                return 0

            lax.fori_loop(0, size // CHUNK, leave, 0)
        return 0

    lax.fori_loop(0, slice_count - mine, backward, 0)

    def emit(i, _):
        rows = pl.ds(pl.multiple_of(i * 16, 16), 16)
        for comp in range(3):
            out[comp, rows, :] = grid[comp, rows, :].astype(BF16)
        return 0

    lax.fori_loop(0, out.shape[1] // 16, emit, 0)


def swap_margins(x, dim):
    count, length = (lax.axis_size("tile"), x.shape[dim])
    last = lax.slice_in_dim(x, length - MARGIN, length, axis=dim)
    leading = lax.slice_in_dim(x, 0, MARGIN, axis=dim)
    before = lax.ppermute(last, "tile", ring(count, 1))
    after = lax.ppermute(leading, "tile", ring(count, -1))
    return before, after


def rows_of(held, order, place, first, stop, piece_rows):
    picked = []
    lookup = jnp.array([order.index(j) for j in range(len(order))], jnp.int32)
    for piece in range(first // piece_rows, stop // piece_rows):
        picked.append(lax.dynamic_index_in_dim(held, lookup[piece ^ place], 0, keepdims=False))
    return jnp.concatenate(picked, axis=-2)


def shards(probe_wave, fresnel_rows, fresnel_cols, object_slices, offsets, measured):
    cut_count = lax.axis_size("cuts")
    probe_count = lax.axis_size("probe")
    section = lax.axis_index("cuts")
    place = lax.axis_index("probe")
    owned = object_slices[0]
    own_count = owned.shape[1]
    width_cols = owned.shape[2]
    size = probe_wave.shape[1]
    count = offsets.shape[1]
    piece_rows = own_count // probe_count
    bits = [1 << b for b in range(probe_count.bit_length() - 1)]

    own = owned.astype(BF16)
    own_top, own_bottom = swap_margins(own, 1)
    piece = lax.dynamic_slice_in_dim(own, place * piece_rows, piece_rows, axis=1)

    reals, imags, tops, bottoms = [], [], [], []
    for _ in range(cut_count - 1):
        piece = lax.ppermute(piece, "cuts", ring(cut_count, 1))
        real, order_a = spread(piece[0], bits)
        imag, order_b = spread(piece[1], bits[::-1])
        last = [
            rows_of(h, o, place, own_count - MARGIN, own_count, piece_rows)
            for h, o in ((real, order_a), (imag, order_b))
        ]
        lead = [
            rows_of(h, o, place, 0, MARGIN, piece_rows)
            for h, o in ((real, order_a), (imag, order_b))
        ]
        tiles = lax.axis_size("tile")
        tops.append(lax.ppermute(jnp.stack(last), "tile", ring(tiles, 1)))
        bottoms.append(lax.ppermute(jnp.stack(lead), "tile", ring(tiles, -1)))
        reals.append(real)
        imags.append(imag)

    row_real, row_imag = (fresnel_rows[0], fresnel_rows[1])
    col_real, col_imag = (fresnel_cols[0], fresnel_cols[1])
    row_mat = jnp.concatenate(
        [
            jnp.concatenate([row_real, -row_imag], axis=1),
            jnp.concatenate([row_imag, row_real], axis=1),
        ],
        axis=0,
    )
    col_mat_t = jnp.concatenate(
        [
            jnp.concatenate([col_real, -col_imag], axis=1),
            jnp.concatenate([col_imag, col_real], axis=1),
        ],
        axis=0,
    )

    info = jnp.stack([section, place]).astype(jnp.int32)
    anywhere = pl.BlockSpec(memory_space=pl.ANY)
    scalars = pl.BlockSpec(memory_space=pltpu.SMEM)
    tall = own_count + 2 * MARGIN
    grid = pl.pallas_call(
        functools.partial(body, tuple(order_a), tuple(order_b), cut_count),
        out_shape=jax.ShapeDtypeStruct((3, tall, width_cols), BF16),
        in_specs=[scalars, scalars] + [anywhere] * 13,
        out_specs=pl.BlockSpec(memory_space=pltpu.VMEM),
        scratch_shapes=[
            pltpu.VMEM((2, 2, tall + ALIGN, width_cols), BF16),
            pltpu.VMEM((cut_count, count, 2, size, size), BF16),
            pltpu.VMEM((count, 2, size, size), BF16),
            pltpu.VMEM((count, size, 2 * size), BF16),
            pltpu.VMEM((count, 2 * size, size), BF16),
            pltpu.VMEM((count, 2 * size, size), BF16),
            pltpu.VMEM((count, size, size), F32),
            pltpu.VMEM((2, size, size), BF16),
            pltpu.VMEM((4, 2 * size, 2 * size), BF16),
            pltpu.VMEM((3, tall + 8, width_cols), F32),
            pltpu.SemaphoreType.DMA((2,)),
            pltpu.SemaphoreType.DMA((4,)),
            pltpu.SemaphoreType.DMA((2,)),
        ],
        compiler_params=pltpu.CompilerParams(vmem_limit_bytes=62 * 1024 * 1024),
        name="gradient",
    )(
        info,
        offsets[0],
        own,
        own_top,
        own_bottom,
        jnp.stack(reals),
        jnp.stack(imags),
        jnp.stack(tops),
        jnp.stack(bottoms),
        probe_wave,
        row_mat,
        row_mat.T,
        col_mat_t.T,
        col_mat_t,
        measured[0],
    )

    tiles = lax.axis_size("tile")
    inside = grid[:, MARGIN : MARGIN + own_count]
    upper = lax.ppermute(grid[:, MARGIN + own_count :], "tile", ring(tiles, 1))
    lower = lax.ppermute(grid[:, :MARGIN], "tile", ring(tiles, -1))
    folded = jnp.concatenate(
        [
            inside[:, :MARGIN].astype(F32) + upper.astype(F32),
            inside[:, MARGIN : own_count - MARGIN].astype(F32),
            inside[:, own_count - MARGIN :].astype(F32) + lower.astype(F32),
        ],
        axis=1,
    ).astype(BF16)

    def rows_for(index):
        return lax.dynamic_slice_in_dim(folded, index * piece_rows, piece_rows, axis=1)

    summed = rows_for(place).astype(F32)
    for j in range(1, probe_count):
        arrived = lax.ppermute(rows_for(place ^ j), "probe", swapped(probe_count, j))
        summed = summed + arrived.astype(F32)
    own_part = lax.dynamic_slice_in_dim(owned, place * piece_rows, piece_rows, 1)
    updated = own_part - summed[:2] / (summed[2] + 1.0)
    return updated[None]


def solution(mesh):
    in_specs = (
        P(),
        P(),
        P(),
        P("cuts", None, "tile", None),
        P("tile", "probe", None),
        P("tile", "probe", None, None),
    )
    out_specs = P("cuts", None, ("tile", "probe"), None)
    return jax.shard_map(shards, mesh=mesh, in_specs=in_specs, out_specs=out_specs, check_vma=False)
```

```python
import functools

import jax
import jax.numpy as jnp
from jax import lax
from jax.experimental import pallas as pl
from jax.experimental.pallas import tpu as pltpu
from jax.sharding import PartitionSpec as P

MARGIN = 128
LANES = 128
CHUNK = 64
ALIGN = 16
F32 = jnp.float32
BF16 = jnp.bfloat16
VMEM_LIMIT = 62 * 1024 * 1024


def ring(count, by):
    return [(i, (i + by) % count) for i in range(count)]


def swapped(x, axis, bit):
    return lax.ppermute(x, axis, [(i, i ^ bit) for i in range(lax.axis_size(axis))])


def low_bit(j):
    return j & -j


def high_bit(j):
    return 1 << (j.bit_length() - 1)


def spread(piece):
    count = lax.axis_size("probe")
    whole = {0: piece}
    for i in range(1, count):
        if low_bit(i) == i:
            whole[i] = swapped(piece, "probe", i)
    real = {i: value[0] for i, value in whole.items()}
    imag = {i: value[1] for i, value in whole.items()}
    held = []
    for i in range(count):
        if i in whole:
            held.append((whole[i],))
        else:
            real[i] = swapped(real[i ^ high_bit(i)], "probe", high_bit(i))
            imag[i] = swapped(imag[i ^ low_bit(i)], "probe", low_bit(i))
            held.append((real[i], imag[i]))
    return held


def dot(a, b):
    return jnp.dot(a, b, preferred_element_type=F32)


def into_rows(parts, target, first, rows, sem):
    span = pl.ds(first, rows)
    if len(parts) == 1:
        return [pltpu.make_async_copy(parts[0], target.at[:, span, :], sem)]
    return [
        pltpu.make_async_copy(part, target.at[comp, span, :], sem)
        for comp, part in enumerate(parts)
    ]


def nested(structure, flat):
    refs = iter(flat)
    return [tuple(next(refs) for _ in range(n)) for n in structure]


def pick_body(structure, info, *refs):
    held = nested(structure, refs)
    out, sem = refs[-2:]
    place = info[1]
    piece_rows = held[0][0].shape[-2]
    count = len(held)
    needed = MARGIN // piece_rows
    for act in (True, False):
        for i, parts in enumerate(held):
            index = place ^ i
            for edge, begin in ((0, count - needed), (1, 0)):

                @pl.when((index >= begin) & (index < begin + needed))
                def _():
                    first = pl.multiple_of((index - begin) * piece_rows, ALIGN)
                    for copy in into_rows(parts, out.at[edge], first, piece_rows, sem.at[0]):
                        copy.start() if act else copy.wait()


def edges(info, held):
    flat = [part for parts in held for part in parts]
    width = flat[0].shape[-1]
    return pl.pallas_call(
        functools.partial(pick_body, tuple(len(parts) for parts in held)),
        out_shape=jax.ShapeDtypeStruct((2, 2, MARGIN, width), BF16),
        in_specs=[pl.BlockSpec(memory_space=pltpu.SMEM)]
        + [pl.BlockSpec(memory_space=pl.ANY)] * len(flat),
        out_specs=pl.BlockSpec(memory_space=pltpu.VMEM),
        scratch_shapes=[pltpu.SemaphoreType.DMA((1,))],
        compiler_params=pltpu.CompilerParams(vmem_limit_bytes=8 * 1024 * 1024),
        cost_estimate=pl.CostEstimate(flops=0, bytes_accessed=1 << 21, transcendentals=0),
        name="edges",
    )(info, *flat)


def across_tiles(both):
    tiles = lax.axis_size("tile")
    if tiles == 2:
        moved = lax.ppermute(both, "tile", ring(tiles, 1))
        return (moved,)
    return (
        lax.ppermute(both[0], "tile", ring(tiles, 1)),
        lax.ppermute(both[1], "tile", ring(tiles, -1)),
    )


def run_body(final, structure, slice_count, info, starts, *refs):
    held_structure, margin_count = structure
    refs = list(refs)

    def take(n):
        taken = refs[:n]
        del refs[:n]
        return taken

    own = take(1)[0]
    margins = [take(margin_count) for _ in range(len(held_structure) + 1)]
    slots = [nested(shape, take(sum(shape))) for shape in held_structure]
    mat_sources = take(4 if final else 2)
    if final:
        begun_wave, begun_wins, begun_saved, measured = take(4)
        out = take(1)[0]
        wave, saved = take(2)
    else:
        probe = take(1)[0]
        wave, wins_out, saved = take(3)
    stage, wins, work, middle, mats = take(5)
    if final:
        amplitude, grid = take(2)
    else:
        probe_v = take(1)[0]
    sem_stage, sem_mat, sem_in = take(3)

    mine, place = info[0], info[1]
    k_first, k_last = (info[2], slice_count) if final else (0, info[2])
    count, size = wave.shape[0], wave.shape[2]
    own_rows, width = own.shape[1], own.shape[2]
    tall = own_rows + 2 * MARGIN
    pieces = len(held_structure[0])
    piece_rows = own_rows // pieces
    lanes = size + LANES
    col_last = (width - size) // LANES - 1
    steps = size // CHUNK

    def stage_start(k):
        slot = lax.rem(k, 2)
        target = stage.at[slot]
        sem = sem_stage.at[slot]

        def margins_in(j):
            if margin_count == 1:
                above, below = margins[j][0].at[0], margins[j][0].at[1]
            else:
                above, below = margins[j]
            return into_rows((above,), target, 0, MARGIN, sem) + into_rows(
                (below,), target, MARGIN + own_rows, MARGIN, sem
            )

        @pl.when((k ^ mine) == 0)
        def _():
            for copy in margins_in(0) + into_rows((own,), target, MARGIN, own_rows, sem):
                copy.start()

        for j in range(1, len(slots) + 1):

            @pl.when((k ^ mine) == j)
            def _():
                for copy in margins_in(j):
                    copy.start()
                for i, parts in enumerate(slots[j - 1]):
                    first = pl.multiple_of(MARGIN + (place ^ i) * piece_rows, ALIGN)
                    for copy in into_rows(parts, target, first, piece_rows, sem):
                        copy.start()

    def stage_wait(k):
        slot = lax.rem(k, 2)
        whole = stage.at[slot, :, pl.ds(0, tall), :]
        pltpu.make_async_copy(whole, whole, sem_stage.at[slot]).wait()

    def span(i, rows=CHUNK, offset=0):
        return pl.ds(pl.multiple_of(i * rows + offset, 8), rows)

    mat_copies = [
        pltpu.make_async_copy(source, mats.at[i], sem_mat.at[i])
        for i, source in enumerate(mat_sources)
    ]

    @pl.when(k_first < k_last)
    def _():
        stage_start(jnp.int32(k_first))

    if final:
        wave_copy = pltpu.make_async_copy(begun_wave, wave, sem_in.at[0])
        saved_copy = pltpu.make_async_copy(begun_saved, saved, sem_in.at[1])
        measured_copy = pltpu.make_async_copy(measured, amplitude, sem_in.at[2])
        wave_copy.start()
    else:
        probe_copy = pltpu.make_async_copy(probe, probe_v, sem_in.at[0])
        probe_copy.start()
    for copy in mat_copies[:2]:
        copy.start()
    if final:
        saved_copy.start()
        measured_copy.start()
        for copy in mat_copies[2:]:
            copy.start()

        def wins_start(k, _):
            pltpu.make_async_copy(begun_wins.at[k], wins.at[k], sem_in.at[3]).start()
            return 0

        def wins_wait(k, _):
            pltpu.make_async_copy(begun_wins.at[k], wins.at[k], sem_in.at[3]).wait()
            return 0

        lax.fori_loop(0, k_first, wins_start, 0)

        def clear(i, _):
            for comp in range(3):
                grid[comp, span(i, 8), :] = jnp.zeros((8, width), F32)
            return 0

        lax.fori_loop(0, grid.shape[1] // 8, clear, 0)
        wave_copy.wait()
        saved_copy.wait()
    else:
        probe_copy.wait()

        def fill(i, _):
            for comp in range(2):
                value = probe_v[comp, span(i), :]
                for position in range(count):
                    wave[position, span(i, CHUNK, comp * size), :] = value
            return 0

        lax.fori_loop(0, steps, fill, 0)

    def column(position):
        col = starts[position, 1]
        tile = jnp.minimum(col // LANES, col_last)
        return pl.multiple_of(tile * LANES, LANES), col - tile * LANES

    def rolled_rows(x, shift, keep):
        groups = x.shape[0] // 8
        turned = pltpu.roll(x.reshape(groups, 8, x.shape[1]), lax.rem(8 - shift, 8), 1)
        row = lax.broadcasted_iota(jnp.int32, (1, 8, x.shape[1]), 1)
        kept = keep // 8
        return jnp.where(row < 8 - shift, turned[:kept], turned[1 : kept + 1]).reshape(
            keep, x.shape[1]
        )

    def rolled_lanes(x, shift):
        back = lax.rem(LANES - shift, LANES)
        tiles = [x[:, j * LANES : (j + 1) * LANES] for j in range(x.shape[1] // LANES)]
        turned = [pltpu.roll(tile, back, 1) for tile in tiles]
        lane = lax.broadcasted_iota(jnp.int32, (1, LANES), 1)
        mask = lane < LANES - shift
        return jnp.concatenate(
            [jnp.where(mask, a, b) for a, b in zip(turned[:-1], turned[1:])], axis=1
        )

    def spread_lanes(x, shift):
        turn = lax.rem(shift, LANES)
        tiles = [x[:, j * LANES : (j + 1) * LANES] for j in range(x.shape[1] // LANES)]
        turned = [pltpu.roll(tile, turn, 1) for tile in tiles]
        lane = lax.broadcasted_iota(jnp.int32, (1, LANES), 1)
        mask = lane < shift
        nothing = jnp.zeros_like(turned[0])
        return jnp.concatenate(
            [jnp.where(mask, a, b) for a, b in zip([nothing] + turned, turned + [nothing])], axis=1
        )

    def spread_rows(x, shift):
        groups = x.shape[0] // 8
        turned = pltpu.roll(x.reshape(groups, 8, x.shape[1]), shift, 1)
        nothing = jnp.zeros((1, 8, x.shape[1]), F32)
        row = lax.broadcasted_iota(jnp.int32, (1, 8, x.shape[1]), 1)
        return jnp.where(
            row < shift,
            jnp.concatenate([nothing, turned], axis=0),
            jnp.concatenate([turned, nothing], axis=0),
        ).reshape(x.shape[0] + 8, x.shape[1])

    def add_piece(position, comp, i, value):
        row = starts[position, 0] + i * CHUNK
        inside = lax.rem(row, 8)
        first = pl.multiple_of(row - inside, 8)
        col_first, shift = column(position)
        wide = spread_lanes(value, shift)
        grid[comp, pl.ds(first, CHUNK + 8), pl.ds(col_first, lanes)] += spread_rows(wide, inside)

    def halves(position, i):
        return (
            wave[position, span(i), :].astype(F32),
            wave[position, span(i, CHUNK, size), :].astype(F32),
        )

    def put_work(position, i, real, imag):
        work[position, span(i), pl.ds(0, size)] = real.astype(BF16)
        work[position, span(i), pl.ds(size, size)] = imag.astype(BF16)

    def propagate(position, col, row):
        for n in range(2):
            part = dot(work[position], mats[col, :, pl.ds(n * size, size)])
            middle[position, pl.ds(n * size, size), :] = part.astype(BF16)
        for m in range(2):
            part = dot(mats[row, pl.ds(m * size, size), :], middle[position])
            wave[position, pl.ds(m * size, size), :] = part.astype(BF16)

    def forward(k, _):
        slot = lax.rem(k, 2)
        stage_wait(k)

        @pl.when(k + 1 < k_last)
        def _():
            stage_start(k + 1)

        @pl.when(k == mine)
        def _():
            for position in range(count):
                for comp in range(2):
                    rows = pl.ds(comp * size, size)
                    saved[position, rows, :] = wave[position, rows, :]

        for position in range(count):
            row_start = starts[position, 0]
            col_first, shift = column(position)
            inside = lax.rem(row_start, ALIGN)
            fine = lax.rem(inside, 8)
            lower = inside >= 8

            def enter(i, _):
                first = pl.multiple_of(row_start - inside + i * CHUNK, ALIGN)

                def window(comp):
                    block = stage[
                        slot, comp, pl.ds(first, CHUNK + ALIGN), pl.ds(col_first, lanes)
                    ].astype(F32)
                    block = jnp.where(lower, block[8:], block[:-8])
                    return rolled_lanes(rolled_rows(block, fine, CHUNK), shift)

                win_real, win_imag = window(0), window(1)
                wins[k, position, 0, span(i), :] = win_real.astype(BF16)
                wins[k, position, 1, span(i), :] = win_imag.astype(BF16)
                real, imag = halves(position, i)
                put_work(
                    position,
                    i,
                    real * win_real - imag * win_imag,
                    real * win_imag + imag * win_real,
                )
                return 0

            lax.fori_loop(0, steps, enter, 0)

        if not final:
            pltpu.make_async_copy(wins.at[k], wins_out.at[k], sem_in.at[1]).start()

        @pl.when(k == k_first)
        def _():
            mat_copies[0].wait()
            mat_copies[1].wait()

        for position in range(count):
            propagate(position, 0, 1)
        return 0

    lax.fori_loop(k_first, k_last, forward, 0)

    if not final:

        @pl.when(k_last == 0)
        def _():
            mat_copies[0].wait()
            mat_copies[1].wait()

        def wins_sent(k, _):
            pltpu.make_async_copy(wins.at[k], wins_out.at[k], sem_in.at[1]).wait()
            return 0

        lax.fori_loop(0, k_last, wins_sent, 0)
        return

    measured_copy.wait()

    for position in range(count):

        def detect(i, _):
            real, imag = halves(position, i)
            seen = amplitude[position, span(i), :]
            factor = 1.0 - seen / jnp.sqrt(real * real + imag * imag + 1.0)
            put_work(position, i, real * factor, imag * factor)
            return 0

        lax.fori_loop(0, steps, detect, 0)

    mat_copies[2].wait()
    mat_copies[3].wait()
    lax.fori_loop(0, k_first, wins_wait, 0)

    def backward(step, _):
        k = slice_count - 1 - step
        for position in range(count):
            propagate(position, 2, 3)
        for position in range(count):

            @pl.when(k == mine)
            def _():
                def collect(i, _):
                    real, imag = halves(position, i)
                    old_real = saved[position, span(i), :].astype(F32)
                    old_imag = saved[position, span(i, CHUNK, size), :].astype(F32)
                    add_piece(position, 0, i, old_real * real + old_imag * imag)
                    add_piece(position, 1, i, old_real * imag - old_imag * real)
                    add_piece(position, 2, i, old_real * old_real + old_imag * old_imag)
                    return 0

                lax.fori_loop(0, steps, collect, 0)

            @pl.when(k != mine)
            def _():
                def leave(i, _):
                    real, imag = halves(position, i)
                    win_real = wins[k, position, 0, span(i), :].astype(F32)
                    win_imag = wins[k, position, 1, span(i), :].astype(F32)
                    put_work(
                        position,
                        i,
                        win_real * real + win_imag * imag,
                        win_real * imag - win_imag * real,
                    )
                    return 0

                lax.fori_loop(0, steps, leave, 0)

        return 0

    lax.fori_loop(0, slice_count - mine, backward, 0)

    def emit(i, _):
        for comp in range(3):
            out[comp, span(i, ALIGN), :] = grid[comp, span(i, ALIGN), :].astype(BF16)
        return 0

    lax.fori_loop(0, tall // ALIGN, emit, 0)


def block_matrix(real, imag):
    return jnp.concatenate(
        [jnp.concatenate([real, -imag], axis=1), jnp.concatenate([imag, real], axis=1)], axis=0
    )


def prefix_ready(section, slots, slice_count):
    ready, total = jnp.int32(1), jnp.int32(0)
    for k in range(slice_count):
        ready = ready * ((section ^ k) <= slots).astype(jnp.int32)
        total = total + ready
    return total


def scattered(folded, place, order):
    bits = len(order)
    rows = folded.shape[1] >> bits
    held = folded.reshape((folded.shape[0],) + (2,) * bits + (rows, folded.shape[2]))
    axes = {bit: 1 + bits - 1 - bit for bit in order}
    for bit in order:
        axis = axes.pop(bit)
        axes = {b: a - (a > axis) for b, a in axes.items()}
        side = (place >> bit) & 1
        mine = lax.dynamic_index_in_dim(held, side, axis, keepdims=False)
        other = lax.dynamic_index_in_dim(held, 1 - side, axis, keepdims=False)
        arrived = swapped(other.astype(BF16), "probe", 1 << bit)
        held = mine.astype(F32) + arrived.astype(F32)
    return held


def shards(probe_wave, fresnel_rows, fresnel_cols, object_slices, offsets, measured):
    cut_count = lax.axis_size("cuts")
    probe_count = lax.axis_size("probe")
    section = lax.axis_index("cuts")
    place = lax.axis_index("probe")
    owned = object_slices[0]
    own_count = owned.shape[1]
    width_cols = owned.shape[2]
    size = probe_wave.shape[1]
    count = offsets.shape[1]
    piece_rows = own_count // probe_count
    tall = own_count + 2 * MARGIN

    first_piece = lax.dynamic_slice_in_dim(owned, place * piece_rows, piece_rows, axis=1)
    first_piece = first_piece.astype(BF16)
    early_slots = max(cut_count - 2, 1)
    info = jnp.stack([section, place, prefix_ready(section, early_slots, cut_count)])
    info = info.astype(jnp.int32)
    slots = {0: first_piece}
    for j in range(1, cut_count):
        slots[j] = swapped(slots[j ^ low_bit(j)], "cuts", low_bit(j))
    own = owned.astype(BF16)
    own_edges = jnp.stack([own[:, own_count - MARGIN :], own[:, :MARGIN]])
    margins = [across_tiles(own_edges)]
    helds = []
    for j in range(1, cut_count):
        held = spread(slots[j])
        margins.append(across_tiles(edges(info, held)))
        helds.append(held)

    row_mat = block_matrix(fresnel_rows[0], fresnel_rows[1])
    col_mat_t = block_matrix(fresnel_cols[0], fresnel_cols[1])
    row_mat_t, col_mat = row_mat.T, col_mat_t.T

    anywhere = pl.BlockSpec(memory_space=pl.ANY)
    scalars = pl.BlockSpec(memory_space=pltpu.SMEM)
    vmem = pl.BlockSpec(memory_space=pltpu.VMEM)
    wave_shape = jax.ShapeDtypeStruct((count, 2 * size, size), BF16)
    prop_flops = 2 * count * 2 * (2 * size) ** 2 * size
    scratch = [
        pltpu.VMEM((2, 2, tall + ALIGN, width_cols), BF16),
        pltpu.VMEM((cut_count, count, 2, size, size), BF16),
        pltpu.VMEM((count, size, 2 * size), BF16),
        pltpu.VMEM((count, 2 * size, size), BF16),
    ]

    def run(final, used, extra, out_shape, out_specs, more, props):
        structure = tuple(tuple(len(parts) for parts in held) for held in helds[:used])
        inputs = [own] + [m for group in margins[: used + 1] for m in group]
        inputs += [part for held in helds[:used] for parts in held for part in parts]
        inputs += extra
        return pl.pallas_call(
            functools.partial(run_body, final, (structure, len(margins[0])), cut_count),
            out_shape=out_shape,
            in_specs=[scalars, scalars] + [anywhere] * len(inputs),
            out_specs=out_specs,
            scratch_shapes=more
            + [pltpu.SemaphoreType.DMA((2,)), pltpu.SemaphoreType.DMA((4,)), pltpu.SemaphoreType.DMA((4,))],
            compiler_params=pltpu.CompilerParams(vmem_limit_bytes=VMEM_LIMIT),
            cost_estimate=pl.CostEstimate(
                flops=props * prop_flops, bytes_accessed=1 << 24, transcendentals=0
            ),
            name="finish" if final else "begin",
        )(info, offsets[0], *inputs)

    wave, wins, saved = run(
        False,
        early_slots,
        [col_mat, row_mat, probe_wave],
        (
            wave_shape,
            jax.ShapeDtypeStruct((cut_count, count, 2, size, size), BF16),
            wave_shape,
        ),
        (vmem, anywhere, vmem),
        scratch
        + [pltpu.VMEM((2, 2 * size, 2 * size), BF16), pltpu.VMEM((2, size, size), BF16)],
        early_slots + 1,
    )
    grid = run(
        True,
        cut_count - 1,
        [col_mat, row_mat, col_mat_t, row_mat_t, wave, wins, saved, measured[0]],
        jax.ShapeDtypeStruct((3, tall, width_cols), BF16),
        vmem,
        [pltpu.VMEM(wave_shape.shape, BF16), pltpu.VMEM(wave_shape.shape, BF16)]
        + scratch
        + [
            pltpu.VMEM((4, 2 * size, 2 * size), BF16),
            pltpu.VMEM((count, size, size), F32),
            pltpu.VMEM((3, tall + 8, width_cols), F32),
        ],
        cut_count + 1,
    )

    tiles = lax.axis_size("tile")
    inside = grid[:, MARGIN : MARGIN + own_count]
    upper = lax.ppermute(grid[:, MARGIN + own_count :], "tile", ring(tiles, 1))
    lower = lax.ppermute(grid[:, :MARGIN], "tile", ring(tiles, -1))
    folded = jnp.concatenate(
        [
            inside[:, :MARGIN].astype(F32) + upper.astype(F32),
            inside[:, MARGIN : own_count - MARGIN].astype(F32),
            inside[:, own_count - MARGIN :].astype(F32) + lower.astype(F32),
        ],
        axis=1,
    ).astype(BF16)

    bits = list(range(probe_count.bit_length() - 1))
    half = width_cols // 2
    left = scattered(folded[:, :, :half], place, bits[::-1])
    right = scattered(folded[:, :, half:], place, bits)
    summed = jnp.concatenate([left, right], axis=-1)
    own_part = lax.dynamic_slice_in_dim(owned, place * piece_rows, piece_rows, 1)
    updated = own_part - summed[:2] / (summed[2] + 1.0)
    return updated[None]


def solution(mesh):
    in_specs = (
        P(),
        P(),
        P(),
        P("cuts", None, "tile", None),
        P("tile", "probe", None),
        P("tile", "probe", None, None),
    )
    out_specs = P("cuts", None, ("tile", "probe"), None)
    return jax.shard_map(shards, mesh=mesh, in_specs=in_specs, out_specs=out_specs, check_vma=False)
```
